32 devices in a mesh: row: 8 (over y, x, core), col: 4 (over z).
Axes of the slice: x: 2, y: 2, z: 4, core: 2. Of those that a mesh axis runs over, the one named last changes fastest.
Arguments:
- pixels: float32 [8, 3, 1024, 2048], P(None, None, 'row', 'col'), may hold values from -6 to 6
- factor: float32 [1024, 512], P('row'), may hold values from -6 to 6
Outputs:
- gram: float32 [1024, 1024], P('row', 'col')
- projected: float32 [1024, 512], P('col', 'row')
The draws below stay inside these ranges and needn't reach their ends.
All inputs are finite; a program needn't handle non-finite values.
Results may differ from the reference program's by a relative error of at most 0.000075.
Values sent between devices are 32-bit elements; how exact they have to be, the bound alone decides.
A program may use at most 64 MiB of HBM per device.

```python
import jax
import jax.numpy as jnp
from jax import lax

H = 1024
W = 2048
C = 3
R = 512
VIEWS = 8


def levels(stream_key, dims, pieces, low, top_value):
    gain, own = 1.0, jax.random.fold_in(stream_key, 6)
    for axis_at, blocks in pieces:
        heights = jnp.exp(jax.random.uniform(jax.random.fold_in(own, axis_at), (blocks,), jnp.float32, low / len(pieces), top_value / len(pieces)))
        gain = gain * jnp.repeat(heights, dims[axis_at] // blocks).reshape([-1 if axis == axis_at else 1 for axis in range(len(dims))])
    return gain


def noise(rng, dims, spread, most, shards=(), kind=jnp.bfloat16):
    values = jax.random.normal(rng, dims, jnp.float32) * spread
    if len(shards) > 0:
        values = levels(rng, dims, shards, -0.22, 0.18) * values
    return jnp.clip(values, min=-most, max=most).astype(kind)


def setup_inputs(seed: int = 0) -> dict:
    streams_of = jax.random.split(jax.random.key(seed), 3)
    pixels = noise(streams_of[0], (VIEWS, C, H, W), 1.0, 6.0, ((2, 8), (3, 4)), jnp.float32)
    factor = noise(streams_of[1], (H, R), 1.0, 6.0, ((0, 8),), jnp.float32)
    return {"pixels": pixels, "factor": factor}


def reference(pixels, factor):
    unfolded = jnp.transpose(pixels, (2, 0, 1, 3)).reshape(H, VIEWS * C * W)
    gram = jnp.dot(unfolded, unfolded.T, precision=lax.Precision.HIGHEST, preferred_element_type=jnp.float32)
    gram = gram / jnp.float32(VIEWS * C * W)
    projected = jnp.dot(gram.T, factor, precision=lax.Precision.HIGHEST, preferred_element_type=jnp.float32)
    return gram, projected
```

```python
import functools

import jax
import jax.numpy as jnp
from jax import lax
from jax.experimental import pallas as pl
from jax.experimental.pallas import tpu as pltpu
from jax.sharding import PartitionSpec as P

MESH = pl.DeviceIdType.MESH


def flip(value, mask, bits):
    out = 0
    for b in range(bits):
        bit = (value // (1 << b)) % 2
        out = out + (1 << b) * ((1 - bit) if (mask >> b) & 1 else bit)
    return out


def differ(left, right, bits):
    out = 0
    for b in range(bits):
        out = out + (1 << b) * (((left // (1 << b)) + (right // (1 << b))) % 2)
    return out


def dot_t(a, b):
    return lax.dot_general(a, b, (((1,), (1,)), ((), ())), preferred_element_type=jnp.float32)


def kernel(
    rows, cols, scale,
    pix, fac, gram, proj,
    xs, hi, lo, part, pair_in, summed, z_in, plane_out, plane_in, term, term_in,
    own_sem, a_send, a_recv, p_send, p_recv, z_send, z_recv, g_send, g_recv, t_send, t_recv,
):
    r = lax.axis_index("row")
    z = lax.axis_index("col")
    core = r % 2
    chip = r // 2
    rbits = rows.bit_length() - 1
    zbits = cols.bit_length() - 1
    chips = rows // 2
    per = pix.shape[0] // rows
    block = pix.shape[1]
    depth = pix.shape[2]
    mate = [flip(r, k, rbits) for k in range(rows)]

    barrier = pltpu.get_barrier_semaphore()
    for k in range(1, rows):
        pl.semaphore_signal(barrier, inc=1, device_id=(mate[k], z), device_id_type=MESH)
    for k in range(1, cols):
        pl.semaphore_signal(barrier, inc=1, device_id=(r, flip(z, k, zbits)), device_id_type=MESH)
    own = pltpu.make_async_copy(pix.at[pl.ds(r * per, per)], xs.at[0], own_sem)
    own.start()
    pl.semaphore_wait(barrier, rows + cols - 2)

    order = sorted(range(1, rows), key=lambda k: (bin(k >> 1).count("1"), k % 2, k))
    a2a = {}
    for k in order:
        a2a[k] = pltpu.make_async_remote_copy(
            src_ref=pix.at[pl.ds(mate[k] * per, per)],
            dst_ref=xs.at[k],
            send_sem=a_send.at[k],
            recv_sem=a_recv.at[k],
            device_id=(mate[k], z),
            device_id_type=MESH,
        )
        a2a[k].start()

    def split(k):
        for p in range(per):
            x = xs[k, p]
            h = x.astype(jnp.bfloat16)
            at = (k // 2, slice((k % 2) * block, (k % 2 + 1) * block), slice(p * depth, (p + 1) * depth))
            hi[at] = h
            lo[at] = (x - h.astype(jnp.float32)).astype(jnp.bfloat16)

    def pair_copy(i, j):
        return pltpu.make_async_remote_copy(
            src_ref=part.at[i, j, 1],
            dst_ref=pair_in.at[i, j],
            send_sem=p_send.at[i, j],
            recv_sem=p_recv.at[i, j],
            device_id=(mate[1], z),
            device_id_type=MESH,
        )

    def z_copy(i, j):
        zt = flip(chip, j, zbits)
        k = differ(z, zt, zbits)
        return zt, pltpu.make_async_remote_copy(
            src_ref=summed.at[i, j],
            dst_ref=z_in.at[k, i],
            send_sem=z_send.at[i, j],
            recv_sem=z_recv.at[k, i],
            device_id=(r, zt),
            device_id_type=MESH,
        )

    def put(i, j, value):
        part[i, j, 0] = value[:block]
        part[i, j, 1] = value[block:]
        pair_copy(i, j).start()

    for g in range(chips):
        for k in (2 * g, 2 * g + 1):
            if k == 0:
                own.wait()
            else:
                a2a[k].wait_recv()
            split(k)
        fresh = []
        for i in range(g):
            value = dot_t(hi[i], hi[g]) + dot_t(hi[i], lo[g]) + dot_t(lo[i], hi[g])
            put(i, g, value)
            put(g, i, value.T)
            fresh += [(i, g), (g, i)]
        put(g, g, dot_t(hi[g], hi[g]) + dot_t(hi[g], lo[g]) + dot_t(lo[g], hi[g]))
        fresh.append((g, g))
        for i, j in fresh:
            pair_copy(i, j).wait_recv()
            summed[i, j, :, :block] = part[i, j, 0, :, :block] + pair_in[i, j, :, block:]
            summed[i, j, :, block:] = part[i, j, 0, :, block:] + pair_in[i, j, :, :block]
            zt, copy = z_copy(i, j)

            @pl.when(zt != z)
            def _():
                copy.start()

    mine = differ(chip, z, zbits)

    def plane_copy(i):
        return pltpu.make_async_remote_copy(
            src_ref=plane_out.at[i],
            dst_ref=plane_in.at[i],
            send_sem=g_send.at[i],
            recv_sem=g_recv.at[i],
            device_id=(mate[2 * i], z),
            device_id_type=MESH,
        )

    for i in list(range(1, chips)) + [0]:
        total = summed[i, mine]
        for k in range(1, cols):
            pltpu.make_async_remote_copy(
                src_ref=summed.at[i, 0],
                dst_ref=z_in.at[k, i],
                send_sem=z_send.at[i, 0],
                recv_sem=z_recv.at[k, i],
                device_id=(r, flip(z, k, zbits)),
                device_id_type=MESH,
            ).wait_recv()
            total = total + z_in[k, i]
        plane_out[i] = total
        if i > 0:
            plane_copy(i).start()
    total = plane_out[0]
    for i in range(1, chips):
        plane_copy(i).wait_recv()
        total = total + plane_in[i]
    total = total * scale
    first = pl.multiple_of(core * block, block)
    second = pl.multiple_of((1 - core) * block, block)
    gram[:, pl.ds(first, block)] = total[:, :block]
    gram[:, pl.ds(second, block)] = total[:, block:]

    value = lax.dot_general(
        fac[...], gram[...], (((0,), (0,)), ((), ())),
        precision=lax.Precision.HIGHEST, preferred_element_type=jnp.float32,
    )
    share = value.shape[0] // rows
    for k in range(rows):
        term[k] = value[k * share:(k + 1) * share]

    def term_copy(k):
        return pltpu.make_async_remote_copy(
            src_ref=term.at[mate[k]],
            dst_ref=term_in.at[k],
            send_sem=t_send.at[k],
            recv_sem=t_recv.at[k],
            device_id=(mate[k], z),
            device_id_type=MESH,
        )

    for k in range(rows - 1, 0, -1):
        term_copy(k).start()
    total = term[r]
    for k in range(1, rows):
        term_copy(k).wait_recv()
        total = total + term_in[k]
    proj[...] = total.T

    for k in range(1, rows):
        a2a[k].wait_send()
        term_copy(k).wait_send()
    for i in range(chips):
        for j in range(chips):
            pair_copy(i, j).wait_send()
            zt, copy = z_copy(i, j)

            @pl.when(zt != z)
            def _():
                copy.wait_send()
        if i > 0:
            plane_copy(i).wait_send()


def fused(pixels, factor):
    rows, cols = lax.axis_size("row"), lax.axis_size("col")
    views, colours, block, depth = pixels.shape
    count = views * colours
    per = count // rows
    chips = rows // 2
    rank = factor.shape[1]
    scale = 1.0 / (count * depth * cols)
    vmem, dma = pltpu.VMEM, pltpu.SemaphoreType.DMA
    f32 = jnp.float32
    return pl.pallas_call(
        functools.partial(kernel, rows, cols, scale),
        out_shape=(
            jax.ShapeDtypeStruct((block, 2 * block), f32),
            jax.ShapeDtypeStruct((2 * block, rank // rows), f32),
        ),
        in_specs=[pl.BlockSpec(memory_space=pl.ANY), pl.BlockSpec(memory_space=pltpu.VMEM)],
        out_specs=(pl.BlockSpec(memory_space=pltpu.VMEM), pl.BlockSpec(memory_space=pltpu.VMEM)),
        scratch_shapes=[
            vmem((rows, per, block, depth), f32),
            vmem((chips, 2 * block, per * depth), jnp.bfloat16),
            vmem((chips, 2 * block, per * depth), jnp.bfloat16),
            vmem((chips, chips, 2, block, 2 * block), f32),
            vmem((chips, chips, block, 2 * block), f32),
            vmem((chips, chips, block, 2 * block), f32),
            vmem((cols, chips, block, 2 * block), f32),
            vmem((chips, block, 2 * block), f32),
            vmem((chips, block, 2 * block), f32),
            vmem((rows, rank // rows, 2 * block), f32),
            vmem((rows, rank // rows, 2 * block), f32),
            dma,
            dma((rows,)), dma((rows,)),
            dma((chips, chips)), dma((chips, chips)),
            dma((chips, chips)), dma((cols, chips)),
            dma((chips,)), dma((chips,)),
            dma((rows,)), dma((rows,)),
        ],
        compiler_params=pltpu.CompilerParams(
            collective_id=0, has_side_effects=True, vmem_limit_bytes=56 * 1024 * 1024
        ),
    )(pixels.reshape(count, block, depth), factor)


def pair_rows(own, others):
    return jnp.einsum(
        "vciw,vcjw->ij", own, others, precision=lax.Precision.HIGHEST, preferred_element_type=jnp.float32
    )


def general(pixels, factor):
    col_count = lax.axis_size("col")
    row_count = lax.axis_size("row")
    weight_scale = 1.0 / (pixels.shape[0] * pixels.shape[1] * pixels.shape[3] * col_count)
    row_block = pixels.shape[2]
    slices = lax.all_to_all(pixels, "row", split_axis=3, concat_axis=2, tiled=True)
    partial_value = pair_rows(slices, slices) * weight_scale
    width = partial_value.shape[0] // col_count
    arranged = partial_value.reshape(row_count, row_block, col_count, width)
    arranged = jnp.transpose(arranged, (0, 2, 1, 3)).reshape(row_count * col_count * row_block, width)
    block = lax.psum_scatter(arranged, ("row", "col"), scatter_dimension=0, tiled=True)
    term = lax.dot_general(
        block, factor, (((0,), (0,)), ((), ())),
        precision=lax.Precision.HIGHEST, preferred_element_type=jnp.float32,
    )
    summed_term = lax.psum(term, "row")
    share = summed_term.shape[1] // row_count
    projected = lax.dynamic_slice_in_dim(summed_term, lax.axis_index("row") * share, share, 1)
    return (block, projected)


def shards(pixels, factor):
    rows, cols = lax.axis_size("row"), lax.axis_size("col")
    views, colours, block, depth = pixels.shape
    fits = (
        rows == 2 * cols
        and rows & (rows - 1) == 0
        and (views * colours) % rows == 0
        and block % 128 == 0
        and depth % 128 == 0
        and factor.shape[1] % (8 * rows) == 0
        and 8 * rows * block * (views * colours // rows) * depth <= 16 * 1024 * 1024
    )
    return (fused if fits else general)(pixels, factor)


def solution(mesh):
    in_specs = (P(None, None, "row", "col"), P("row", None))
    out_specs = (P("row", "col"), P("col", "row"))
    return jax.shard_map(shards, mesh=mesh, in_specs=in_specs, out_specs=out_specs, check_vma=False)
```

```python
import functools

import jax
import jax.numpy as jnp
from jax import lax
from jax.experimental import pallas as pl
from jax.experimental.pallas import tpu as pltpu
from jax.sharding import PartitionSpec as P

MESH = pl.DeviceIdType.MESH


def flip(value, mask, bits):
    out = 0
    for b in range(bits):
        bit = (value // (1 << b)) % 2
        out = out + (1 << b) * ((1 - bit) if (mask >> b) & 1 else bit)
    return out


def differ(left, right, bits):
    out = 0
    for b in range(bits):
        out = out + (1 << b) * (((left // (1 << b)) + (right // (1 << b))) % 2)
    return out


def dot_t(a, b):
    return lax.dot_general(a, b, (((1,), (1,)), ((), ())), preferred_element_type=jnp.float32)


def kernel(
    rows, cols, scale,
    pix, fac, gram, proj,
    xs, hi, lo, part, pair_in, summed, z_in, plane_out, plane_in, late_in, late_sum, zl_in, term, term_in,
    own_sem, a_send, a_recv, p_send, p_recv, z_send, z_recv, g_send, g_recv,
    l_send, l_recv, zl_send, zl_recv, t_send, t_recv,
):
    r = lax.axis_index("row")
    z = lax.axis_index("col")
    core = r % 2
    chip = r // 2
    rbits = rows.bit_length() - 1
    zbits = cols.bit_length() - 1
    chips = rows // 2
    last = chips - 1
    mine = differ(chip, z, zbits)
    per = pix.shape[0] // rows
    block = pix.shape[1]
    depth = pix.shape[2]
    mate = [flip(r, k, rbits) for k in range(rows)]

    barrier = pltpu.get_barrier_semaphore()
    for k in range(1, rows):
        pl.semaphore_signal(barrier, inc=1, device_id=(mate[k], z), device_id_type=MESH)
    for k in range(1, cols):
        pl.semaphore_signal(barrier, inc=1, device_id=(r, flip(z, k, zbits)), device_id_type=MESH)
    own = pltpu.make_async_copy(pix.at[pl.ds(r * per, per)], xs.at[0], own_sem)
    own.start()
    pl.semaphore_wait(barrier, rows + cols - 2)

    order = sorted(range(1, rows), key=lambda k: (bin(k >> 1).count("1"), k % 2, k))
    a2a = {}
    for k in order:
        a2a[k] = pltpu.make_async_remote_copy(
            src_ref=pix.at[pl.ds(mate[k] * per, per)],
            dst_ref=xs.at[k],
            send_sem=a_send.at[k],
            recv_sem=a_recv.at[k],
            device_id=(mate[k], z),
            device_id_type=MESH,
        )
        if k < 2 * last:
            a2a[k].start()

    def split(k):
        for p in range(per):
            x = xs[k, p]
            h = x.astype(jnp.bfloat16)
            at = (k // 2, slice((k % 2) * block, (k % 2 + 1) * block), slice(p * depth, (p + 1) * depth))
            hi[at] = h
            lo[at] = (x - h.astype(jnp.float32)).astype(jnp.bfloat16)

    def pair_copy(i, j):
        return pltpu.make_async_remote_copy(
            src_ref=part.at[i, j, 1],
            dst_ref=pair_in.at[i, j],
            send_sem=p_send.at[i, j],
            recv_sem=p_recv.at[i, j],
            device_id=(mate[1], z),
            device_id_type=MESH,
        )

    def z_copy(i, j):
        zt = flip(chip, j, zbits)
        k = differ(z, zt, zbits)
        return zt, pltpu.make_async_remote_copy(
            src_ref=summed.at[i, j],
            dst_ref=z_in.at[k, i],
            send_sem=z_send.at[i, j],
            recv_sem=z_recv.at[k, i],
            device_id=(r, zt),
            device_id_type=MESH,
        )

    def put(i, j, value):
        part[i, j, 0] = value[:block]
        part[i, j, 1] = value[block:]
        pair_copy(i, j).start()

    def late_copy(i, j):
        return pltpu.make_async_remote_copy(
            src_ref=summed.at[i, j],
            dst_ref=late_in.at[i, i ^ j],
            send_sem=l_send.at[i, i ^ j],
            recv_sem=l_recv.at[i, i ^ j],
            device_id=(mate[2 * i], z),
            device_id_type=MESH,
        )

    def z_late_copy(m):
        zt = flip(chip, m, zbits)
        k = differ(z, zt, zbits)
        return zt, pltpu.make_async_remote_copy(
            src_ref=late_sum.at[m],
            dst_ref=zl_in.at[k],
            send_sem=zl_send.at[m],
            recv_sem=zl_recv.at[k],
            device_id=(r, zt),
            device_id_type=MESH,
        )

    def plane_copy(i):
        return pltpu.make_async_remote_copy(
            src_ref=plane_out.at[i],
            dst_ref=plane_in.at[i],
            send_sem=g_send.at[i],
            recv_sem=g_recv.at[i],
            device_id=(mate[2 * i], z),
            device_id_type=MESH,
        )

    for g in range(chips):
        for k in (2 * g, 2 * g + 1):
            if k == 0:
                own.wait()
            else:
                a2a[k].wait_recv()
            split(k)
        fresh = []
        for i in range(g):
            value = dot_t(hi[i], hi[g]) + dot_t(hi[i], lo[g]) + dot_t(lo[i], hi[g])
            put(g, i, value.T)
            put(i, g, value)
            fresh += [(g, i), (i, g)]
        put(g, g, dot_t(hi[g], hi[g]) + dot_t(hi[g], lo[g]) + dot_t(lo[g], hi[g]))
        fresh.append((g, g))
        if g == 0:
            for k in order:
                if 2 <= k < 2 * last:
                    a2a[k].wait_send()
            for k in (2 * last, 2 * last + 1):
                a2a[k].start()
        for i, j in fresh:
            pair_copy(i, j).wait_recv()
            summed[i, j, :, :block] = part[i, j, 0, :, :block] + pair_in[i, j, :, block:]
            summed[i, j, :, block:] = part[i, j, 0, :, block:] + pair_in[i, j, :, :block]
            if g == last:
                if i > 0:
                    late_copy(i, j).start()
            else:
                zt, copy = z_copy(i, j)

                @pl.when(zt != z)
                def _():
                    copy.start()

    for i in list(range(1, last)) + [0]:
        @pl.when(mine < last)
        def _():
            total = summed[i, mine]
            for k in range(1, cols):
                pltpu.make_async_remote_copy(
                    src_ref=summed.at[i, 0],
                    dst_ref=z_in.at[k, i],
                    send_sem=z_send.at[i, 0],
                    recv_sem=z_recv.at[k, i],
                    device_id=(r, flip(z, k, zbits)),
                    device_id_type=MESH,
                ).wait_recv()
                total = total + z_in[k, i]
            plane_out[i] = total

        @pl.when(mine == last)
        def _():
            plane_out[i] = jnp.zeros((block, 2 * block), jnp.float32)

        if i > 0:
            plane_copy(i).start()

    for m in range(last, -1, -1):
        sources = {last, last ^ m}
        total = None
        for i in sorted(sources):
            if i == 0:
                piece = summed[0, last]
            else:
                late_copy(i, i ^ m).wait_recv()
                piece = late_in[i, m]
            total = piece if total is None else total + piece
        late_sum[m] = total
        zt, copy = z_late_copy(m)

        @pl.when(zt != z)
        def _():
            copy.start()

    total = plane_out[0]
    for i in range(1, last):
        plane_copy(i).wait_recv()
        total = total + plane_in[i]
    total = total + late_sum[mine]
    for k in range(1, cols):
        pltpu.make_async_remote_copy(
            src_ref=late_sum.at[0],
            dst_ref=zl_in.at[k],
            send_sem=zl_send.at[0],
            recv_sem=zl_recv.at[k],
            device_id=(r, flip(z, k, zbits)),
            device_id_type=MESH,
        ).wait_recv()
        total = total + zl_in[k]
    total = total * scale
    first = pl.multiple_of(core * block, block)
    second = pl.multiple_of((1 - core) * block, block)
    gram[:, pl.ds(first, block)] = total[:, :block]
    gram[:, pl.ds(second, block)] = total[:, block:]

    value = lax.dot_general(
        fac[...], gram[...], (((0,), (0,)), ((), ())),
        precision=lax.Precision.HIGHEST, preferred_element_type=jnp.float32,
    )
    share = value.shape[0] // rows
    for k in range(rows):
        term[k] = value[k * share:(k + 1) * share]

    def term_copy(k):
        return pltpu.make_async_remote_copy(
            src_ref=term.at[mate[k]],
            dst_ref=term_in.at[k],
            send_sem=t_send.at[k],
            recv_sem=t_recv.at[k],
            device_id=(mate[k], z),
            device_id_type=MESH,
        )

    for k in range(rows - 1, 0, -1):
        term_copy(k).start()
    total = term[r]
    for k in range(1, rows):
        term_copy(k).wait_recv()
        total = total + term_in[k]
    proj[...] = total.T

    for k in range(1, rows):
        if k < 2 or k >= 2 * last:
            a2a[k].wait_send()
        term_copy(k).wait_send()
    for i in range(chips):
        for j in range(chips):
            pair_copy(i, j).wait_send()
            if i < last and j < last:
                zt, copy = z_copy(i, j)

                @pl.when(zt != z)
                def _():
                    copy.wait_send()
            elif i > 0:
                late_copy(i, j).wait_send()
        if 0 < i < last:
            plane_copy(i).wait_send()
        zt, copy = z_late_copy(i)

        @pl.when(zt != z)
        def _():
            copy.wait_send()


def fused(pixels, factor):
    rows, cols = lax.axis_size("row"), lax.axis_size("col")
    views, colours, block, depth = pixels.shape
    count = views * colours
    per = count // rows
    chips = rows // 2
    rank = factor.shape[1]
    scale = 1.0 / (count * depth * cols)
    vmem, dma = pltpu.VMEM, pltpu.SemaphoreType.DMA
    f32 = jnp.float32
    return pl.pallas_call(
        functools.partial(kernel, rows, cols, scale),
        out_shape=(
            jax.ShapeDtypeStruct((block, 2 * block), f32),
            jax.ShapeDtypeStruct((2 * block, rank // rows), f32),
        ),
        in_specs=[pl.BlockSpec(memory_space=pl.ANY), pl.BlockSpec(memory_space=pltpu.VMEM)],
        out_specs=(pl.BlockSpec(memory_space=pltpu.VMEM), pl.BlockSpec(memory_space=pltpu.VMEM)),
        scratch_shapes=[
            vmem((rows, per, block, depth), f32),
            vmem((chips, 2 * block, per * depth), jnp.bfloat16),
            vmem((chips, 2 * block, per * depth), jnp.bfloat16),
            vmem((chips, chips, 2, block, 2 * block), f32),
            vmem((chips, chips, block, 2 * block), f32),
            vmem((chips, chips, block, 2 * block), f32),
            vmem((cols, chips, block, 2 * block), f32),
            vmem((chips, block, 2 * block), f32),
            vmem((chips, block, 2 * block), f32),
            vmem((chips, chips, block, 2 * block), f32),
            vmem((chips, block, 2 * block), f32),
            vmem((cols, block, 2 * block), f32),
            vmem((rows, rank // rows, 2 * block), f32),
            vmem((rows, rank // rows, 2 * block), f32),
            dma,
            dma((rows,)), dma((rows,)),
            dma((chips, chips)), dma((chips, chips)),
            dma((chips, chips)), dma((cols, chips)),
            dma((chips,)), dma((chips,)),
            dma((chips, chips)), dma((chips, chips)),
            dma((chips,)), dma((cols,)),
            dma((rows,)), dma((rows,)),
        ],
        compiler_params=pltpu.CompilerParams(
            collective_id=0, has_side_effects=True, vmem_limit_bytes=56 * 1024 * 1024
        ),
    )(pixels.reshape(count, block, depth), factor)


def pair_rows(own, others):
    return jnp.einsum(
        "vciw,vcjw->ij", own, others, precision=lax.Precision.HIGHEST, preferred_element_type=jnp.float32
    )


def general(pixels, factor):
    col_count = lax.axis_size("col")
    row_count = lax.axis_size("row")
    weight_scale = 1.0 / (pixels.shape[0] * pixels.shape[1] * pixels.shape[3] * col_count)
    row_block = pixels.shape[2]
    slices = lax.all_to_all(pixels, "row", split_axis=3, concat_axis=2, tiled=True)
    partial_value = pair_rows(slices, slices) * weight_scale
    width = partial_value.shape[0] // col_count
    arranged = partial_value.reshape(row_count, row_block, col_count, width)
    arranged = jnp.transpose(arranged, (0, 2, 1, 3)).reshape(row_count * col_count * row_block, width)
    block = lax.psum_scatter(arranged, ("row", "col"), scatter_dimension=0, tiled=True)
    term = lax.dot_general(
        block, factor, (((0,), (0,)), ((), ())),
        precision=lax.Precision.HIGHEST, preferred_element_type=jnp.float32,
    )
    summed_term = lax.psum(term, "row")
    share = summed_term.shape[1] // row_count
    projected = lax.dynamic_slice_in_dim(summed_term, lax.axis_index("row") * share, share, 1)
    return (block, projected)


def shards(pixels, factor):
    rows, cols = lax.axis_size("row"), lax.axis_size("col")
    views, colours, block, depth = pixels.shape
    fits = (
        rows == 2 * cols
        and rows >= 4
        and rows & (rows - 1) == 0
        and (views * colours) % rows == 0
        and block % 128 == 0
        and depth % 128 == 0
        and factor.shape[1] % (8 * rows) == 0
        and 8 * rows * block * (views * colours // rows) * depth <= 16 * 1024 * 1024
    )
    return (fused if fits else general)(pixels, factor)


def solution(mesh):
    in_specs = (P(None, None, "row", "col"), P("row", None))
    out_specs = (P("row", "col"), P("col", "row"))
    return jax.shard_map(shards, mesh=mesh, in_specs=in_specs, out_specs=out_specs, check_vma=False)
```

```python
import functools

import jax
import jax.numpy as jnp
from jax import lax
from jax.experimental import pallas as pl
from jax.experimental.pallas import tpu as pltpu
from jax.sharding import PartitionSpec as P

MESH = pl.DeviceIdType.MESH


def flip(value, mask, bits):
    out = 0
    for b in range(bits):
        bit = (value // (1 << b)) % 2
        out = out + (1 << b) * ((1 - bit) if (mask >> b) & 1 else bit)
    return out


def differ(left, right, bits):
    out = 0
    for b in range(bits):
        out = out + (1 << b) * (((left // (1 << b)) + (right // (1 << b))) % 2)
    return out


def dot_t(a, b):
    return lax.dot_general(a, b, (((1,), (1,)), ((), ())), preferred_element_type=jnp.float32)


def kernel(
    rows, cols, scale,
    pix, fac, gram, proj,
    xs, hi, lo, part, pair_in, summed, z_in, plane_out, plane_in, late_in, late_sum, zl_in, acc, term, term_in,
    own_sem, a_send, a_recv, d_send, d_recv, p_send, p_recv, z_send, z_recv, g_send, g_recv,
    l_send, l_recv, zl_send, zl_recv, t_send, t_recv,
):
    r = lax.axis_index("row")
    z = lax.axis_index("col")
    core = r % 2
    chip = r // 2
    rbits = rows.bit_length() - 1
    zbits = cols.bit_length() - 1
    chips = rows // 2
    last = chips - 1
    mine = differ(chip, z, zbits)
    per = pix.shape[0] // rows
    block = pix.shape[1]
    depth = pix.shape[2]
    mate = [flip(r, k, rbits) for k in range(rows)]

    barrier = pltpu.get_barrier_semaphore()
    for k in range(1, rows):
        pl.semaphore_signal(barrier, inc=1, device_id=(mate[k], z), device_id_type=MESH)
    for k in range(1, cols):
        pl.semaphore_signal(barrier, inc=1, device_id=(r, flip(z, k, zbits)), device_id_type=MESH)
    own = pltpu.make_async_copy(pix.at[pl.ds(r * per, per)], xs.at[0], own_sem)
    own.start()
    pl.semaphore_wait(barrier, rows + cols - 2)

    order = sorted(range(1, rows), key=lambda k: (bin(k >> 1).count("1"), k % 2, k))
    a2a = {}
    for k in order:
        a2a[k] = [
            pltpu.make_async_remote_copy(
                src_ref=pix.at[pl.ds(mate[k] * per + p, size)],
                dst_ref=xs.at[k, pl.ds(p, size)],
                send_sem=sems[0],
                recv_sem=sems[1],
                device_id=(mate[k], z),
                device_id_type=MESH,
            )
            for p, size, sems in (
                [(0, per, (a_send.at[k], a_recv.at[k]))]
                if k < 2 * last
                else [(p, 1, (d_send.at[k % 2, p], d_recv.at[k % 2, p])) for p in range(per)]
            )
        ]
        if k < 2 * last:
            a2a[k][0].start()

    def split(k, pieces):
        for p in pieces:
            x = xs[k, p]
            h = x.astype(jnp.bfloat16)
            at = (k // 2, slice((k % 2) * block, (k % 2 + 1) * block), slice(p * depth, (p + 1) * depth))
            hi[at] = h
            lo[at] = (x - h.astype(jnp.float32)).astype(jnp.bfloat16)

    def pair_copy(i, j):
        return pltpu.make_async_remote_copy(
            src_ref=part.at[i, j, 1],
            dst_ref=pair_in.at[i, j],
            send_sem=p_send.at[i, j],
            recv_sem=p_recv.at[i, j],
            device_id=(mate[1], z),
            device_id_type=MESH,
        )

    def z_copy(i, j):
        zt = flip(chip, j, zbits)
        k = differ(z, zt, zbits)
        return zt, pltpu.make_async_remote_copy(
            src_ref=summed.at[i, j],
            dst_ref=z_in.at[k, i],
            send_sem=z_send.at[i, j],
            recv_sem=z_recv.at[k, i],
            device_id=(r, zt),
            device_id_type=MESH,
        )

    def put(i, j, value):
        part[i, j, 0] = value[:block]
        part[i, j, 1] = value[block:]
        pair_copy(i, j).start()

    def late_copy(i, j):
        return pltpu.make_async_remote_copy(
            src_ref=summed.at[i, j],
            dst_ref=late_in.at[i, i ^ j],
            send_sem=l_send.at[i, i ^ j],
            recv_sem=l_recv.at[i, i ^ j],
            device_id=(mate[2 * i], z),
            device_id_type=MESH,
        )

    def z_late_copy(m):
        zt = flip(chip, m, zbits)
        k = differ(z, zt, zbits)
        return zt, pltpu.make_async_remote_copy(
            src_ref=late_sum.at[m],
            dst_ref=zl_in.at[k],
            send_sem=zl_send.at[m],
            recv_sem=zl_recv.at[k],
            device_id=(r, zt),
            device_id_type=MESH,
        )

    def plane_copy(i):
        return pltpu.make_async_remote_copy(
            src_ref=plane_out.at[i],
            dst_ref=plane_in.at[i],
            send_sem=g_send.at[i],
            recv_sem=g_recv.at[i],
            device_id=(mate[2 * i], z),
            device_id_type=MESH,
        )

    def finish(i, j):
        pair_copy(i, j).wait_recv()
        summed[i, j, :, :block] = part[i, j, 0, :, :block] + pair_in[i, j, :, block:]
        summed[i, j, :, block:] = part[i, j, 0, :, block:] + pair_in[i, j, :, :block]
        if i == last or j == last:
            if i > 0:
                late_copy(i, j).start()
        else:
            zt, copy = z_copy(i, j)

            @pl.when(zt != z)
            def _():
                copy.start()

    def product(i, g, at):
        return (
            dot_t(hi[i, :, at], hi[g, :, at])
            + dot_t(hi[i, :, at], lo[g, :, at])
            + dot_t(lo[i, :, at], hi[g, :, at])
        )

    for g in range(last):
        for k in (2 * g, 2 * g + 1):
            if k == 0:
                own.wait()
            else:
                a2a[k][0].wait_recv()
            split(k, range(per))
        fresh = []
        for i in range(g + 1):
            value = product(i, g, slice(None))
            put(i, g, value)
            fresh.append((i, g))
            if i < g:
                put(g, i, value.T)
                fresh.append((g, i))
        if g == 0:
            for k in order:
                if 2 <= k < 2 * last:
                    a2a[k][0].wait_send()
            for p in range(per):
                for k in (2 * last, 2 * last + 1):
                    a2a[k][p].start()
        for i, j in fresh:
            finish(i, j)

    for p in range(per):
        for k in (2 * last, 2 * last + 1):
            a2a[k][p].wait_recv()
            split(k, (p,))
        at = slice(p * depth, (p + 1) * depth)
        waiting = []
        for i in range(chips):
            value = product(i, last, at)
            if p > 0:
                value = value + acc[i]
            if p < per - 1:
                acc[i] = value
                continue
            fresh = [(i, last)]
            if i < last:
                put(last, i, value.T)
                fresh.insert(0, (last, i))
            put(i, last, value)
            for pair in waiting:
                finish(*pair)
            waiting = fresh
        for pair in waiting:
            finish(*pair)

    for i in list(range(1, last)) + [0]:
        @pl.when(mine < last)
        def _():
            total = summed[i, mine]
            for k in range(1, cols):
                pltpu.make_async_remote_copy(
                    src_ref=summed.at[i, 0],
                    dst_ref=z_in.at[k, i],
                    send_sem=z_send.at[i, 0],
                    recv_sem=z_recv.at[k, i],
                    device_id=(r, flip(z, k, zbits)),
                    device_id_type=MESH,
                ).wait_recv()
                total = total + z_in[k, i]
            plane_out[i] = total

        @pl.when(mine == last)
        def _():
            plane_out[i] = jnp.zeros((block, 2 * block), jnp.float32)

        if i > 0:
            plane_copy(i).start()

    for m in range(last, -1, -1):
        sources = {last, last ^ m}
        total = None
        for i in sorted(sources):
            if i == 0:
                piece = summed[0, last]
            else:
                late_copy(i, i ^ m).wait_recv()
                piece = late_in[i, m]
            total = piece if total is None else total + piece
        late_sum[m] = total
        zt, copy = z_late_copy(m)

        @pl.when(zt != z)
        def _():
            copy.start()

    total = plane_out[0]
    for i in range(1, last):
        plane_copy(i).wait_recv()
        total = total + plane_in[i]
    total = total + late_sum[mine]
    for k in range(1, cols):
        pltpu.make_async_remote_copy(
            src_ref=late_sum.at[0],
            dst_ref=zl_in.at[k],
            send_sem=zl_send.at[0],
            recv_sem=zl_recv.at[k],
            device_id=(r, flip(z, k, zbits)),
            device_id_type=MESH,
        ).wait_recv()
        total = total + zl_in[k]
    total = total * scale
    first = pl.multiple_of(core * block, block)
    second = pl.multiple_of((1 - core) * block, block)
    gram[:, pl.ds(first, block)] = total[:, :block]
    gram[:, pl.ds(second, block)] = total[:, block:]

    value = lax.dot_general(
        fac[...], gram[...], (((0,), (0,)), ((), ())),
        precision=lax.Precision.HIGHEST, preferred_element_type=jnp.float32,
    )
    share = value.shape[0] // rows
    for k in range(rows):
        term[k] = value[k * share:(k + 1) * share]

    def term_copy(k):
        return pltpu.make_async_remote_copy(
            src_ref=term.at[mate[k]],
            dst_ref=term_in.at[k],
            send_sem=t_send.at[k],
            recv_sem=t_recv.at[k],
            device_id=(mate[k], z),
            device_id_type=MESH,
        )

    for k in range(rows - 1, 0, -1):
        term_copy(k).start()
    total = term[r]
    for k in range(1, rows):
        term_copy(k).wait_recv()
        total = total + term_in[k]
    proj[...] = total.T

    for k in range(1, rows):
        if k < 2 or k >= 2 * last:
            for copy in a2a[k]:
                copy.wait_send()
        term_copy(k).wait_send()
    for i in range(chips):
        for j in range(chips):
            pair_copy(i, j).wait_send()
            if i < last and j < last:
                zt, copy = z_copy(i, j)

                @pl.when(zt != z)
                def _():
                    copy.wait_send()
            elif i > 0:
                late_copy(i, j).wait_send()
        if 0 < i < last:
            plane_copy(i).wait_send()
        zt, copy = z_late_copy(i)

        @pl.when(zt != z)
        def _():
            copy.wait_send()


def fused(pixels, factor):
    rows, cols = lax.axis_size("row"), lax.axis_size("col")
    views, colours, block, depth = pixels.shape
    count = views * colours
    per = count // rows
    chips = rows // 2
    rank = factor.shape[1]
    scale = 1.0 / (count * depth * cols)
    vmem, dma = pltpu.VMEM, pltpu.SemaphoreType.DMA
    f32 = jnp.float32
    return pl.pallas_call(
        functools.partial(kernel, rows, cols, scale),
        out_shape=(
            jax.ShapeDtypeStruct((block, 2 * block), f32),
            jax.ShapeDtypeStruct((2 * block, rank // rows), f32),
        ),
        in_specs=[pl.BlockSpec(memory_space=pl.ANY), pl.BlockSpec(memory_space=pltpu.VMEM)],
        out_specs=(pl.BlockSpec(memory_space=pltpu.VMEM), pl.BlockSpec(memory_space=pltpu.VMEM)),
        scratch_shapes=[
            vmem((rows, per, block, depth), f32),
            vmem((chips, 2 * block, per * depth), jnp.bfloat16),
            vmem((chips, 2 * block, per * depth), jnp.bfloat16),
            vmem((chips, chips, 2, block, 2 * block), f32),
            vmem((chips, chips, block, 2 * block), f32),
            vmem((chips, chips, block, 2 * block), f32),
            vmem((cols, chips, block, 2 * block), f32),
            vmem((chips, block, 2 * block), f32),
            vmem((chips, block, 2 * block), f32),
            vmem((chips, chips, block, 2 * block), f32),
            vmem((chips, block, 2 * block), f32),
            vmem((cols, block, 2 * block), f32),
            vmem((chips, 2 * block, 2 * block), f32),
            vmem((rows, rank // rows, 2 * block), f32),
            vmem((rows, rank // rows, 2 * block), f32),
            dma,
            dma((rows,)), dma((rows,)),
            dma((2, per)), dma((2, per)),
            dma((chips, chips)), dma((chips, chips)),
            dma((chips, chips)), dma((cols, chips)),
            dma((chips,)), dma((chips,)),
            dma((chips, chips)), dma((chips, chips)),
            dma((chips,)), dma((cols,)),
            dma((rows,)), dma((rows,)),
        ],
        compiler_params=pltpu.CompilerParams(
            collective_id=0, has_side_effects=True, vmem_limit_bytes=56 * 1024 * 1024
        ),
    )(pixels.reshape(count, block, depth), factor)


def pair_rows(own, others):
    return jnp.einsum(
        "vciw,vcjw->ij", own, others, precision=lax.Precision.HIGHEST, preferred_element_type=jnp.float32
    )


def general(pixels, factor):
    col_count = lax.axis_size("col")
    row_count = lax.axis_size("row")
    weight_scale = 1.0 / (pixels.shape[0] * pixels.shape[1] * pixels.shape[3] * col_count)
    row_block = pixels.shape[2]
    slices = lax.all_to_all(pixels, "row", split_axis=3, concat_axis=2, tiled=True)
    partial_value = pair_rows(slices, slices) * weight_scale
    width = partial_value.shape[0] // col_count
    arranged = partial_value.reshape(row_count, row_block, col_count, width)
    arranged = jnp.transpose(arranged, (0, 2, 1, 3)).reshape(row_count * col_count * row_block, width)
    block = lax.psum_scatter(arranged, ("row", "col"), scatter_dimension=0, tiled=True)
    term = lax.dot_general(
        block, factor, (((0,), (0,)), ((), ())),
        precision=lax.Precision.HIGHEST, preferred_element_type=jnp.float32,
    )
    summed_term = lax.psum(term, "row")
    share = summed_term.shape[1] // row_count
    projected = lax.dynamic_slice_in_dim(summed_term, lax.axis_index("row") * share, share, 1)
    return (block, projected)


def shards(pixels, factor):
    rows, cols = lax.axis_size("row"), lax.axis_size("col")
    views, colours, block, depth = pixels.shape
    fits = (
        rows == 2 * cols
        and rows >= 4
        and rows & (rows - 1) == 0
        and (views * colours) % rows == 0
        and block % 128 == 0
        and depth % 128 == 0
        and factor.shape[1] % (8 * rows) == 0
        and 8 * rows * block * (views * colours // rows) * depth <= 16 * 1024 * 1024
    )
    return (fused if fits else general)(pixels, factor)


def solution(mesh):
    in_specs = (P(None, None, "row", "col"), P("row", None))
    out_specs = (P("row", "col"), P("col", "row"))
    return jax.shard_map(shards, mesh=mesh, in_specs=in_specs, out_specs=out_specs, check_vma=False)
```

```python
import functools

import jax
import jax.numpy as jnp
from jax import lax
from jax.experimental import pallas as pl
from jax.experimental.pallas import tpu as pltpu
from jax.sharding import PartitionSpec as P

MESH = pl.DeviceIdType.MESH


def flip(value, mask, bits):
    out = 0
    for b in range(bits):
        bit = (value // (1 << b)) % 2
        out = out + (1 << b) * ((1 - bit) if (mask >> b) & 1 else bit)
    return out


def differ(left, right, bits):
    out = 0
    for b in range(bits):
        out = out + (1 << b) * (((left // (1 << b)) + (right // (1 << b))) % 2)
    return out


def dot_t(a, b):
    return lax.dot_general(a, b, (((1,), (1,)), ((), ())), preferred_element_type=jnp.float32)


def kernel(
    rows, cols, scale,
    pix, fac, gram, proj,
    xs, hi, lo, part, pair_in, summed, z_in, plane_out, plane_in, late_in, late_sum, zl_in, acc, term, term_in,
    own_sem, a_send, a_recv, d_send, d_recv, p_send, p_recv, z_send, z_recv, g_send, g_recv,
    l_send, l_recv, zl_send, zl_recv, t_send, t_recv,
):
    r = lax.axis_index("row")
    z = lax.axis_index("col")
    core = r % 2
    chip = r // 2
    rbits = rows.bit_length() - 1
    zbits = cols.bit_length() - 1
    chips = rows // 2
    last = chips - 1
    mine = differ(chip, z, zbits)
    per = pix.shape[0] // rows
    block = pix.shape[1]
    depth = pix.shape[2]
    mate = [flip(r, k, rbits) for k in range(rows)]

    barrier = pltpu.get_barrier_semaphore()
    for k in range(1, rows):
        pl.semaphore_signal(barrier, inc=1, device_id=(mate[k], z), device_id_type=MESH)
    for k in range(1, cols):
        pl.semaphore_signal(barrier, inc=1, device_id=(r, flip(z, k, zbits)), device_id_type=MESH)
    own = pltpu.make_async_copy(pix.at[pl.ds(r * per, per)], xs.at[0], own_sem)
    own.start()
    pl.semaphore_wait(barrier, rows + cols - 2)

    order = sorted(range(1, rows), key=lambda k: (bin(k >> 1).count("1"), k % 2, k))
    a2a = {}
    for k in order:
        a2a[k] = [
            pltpu.make_async_remote_copy(
                src_ref=pix.at[pl.ds(mate[k] * per + p, size)],
                dst_ref=xs.at[k, pl.ds(p, size)],
                send_sem=sems[0],
                recv_sem=sems[1],
                device_id=(mate[k], z),
                device_id_type=MESH,
            )
            for p, size, sems in (
                [(0, per, (a_send.at[k], a_recv.at[k]))]
                if k < 2 * last
                else [(p, 1, (d_send.at[k % 2, p], d_recv.at[k % 2, p])) for p in range(per)]
            )
        ]
        if k < 2 * last:
            a2a[k][0].start()

    def split(k, pieces):
        for p in pieces:
            x = xs[k, p]
            h = x.astype(jnp.bfloat16)
            at = (k // 2, slice((k % 2) * block, (k % 2 + 1) * block), slice(p * depth, (p + 1) * depth))
            hi[at] = h
            lo[at] = (x - h.astype(jnp.float32)).astype(jnp.bfloat16)

    def pair_copy(i, j):
        return pltpu.make_async_remote_copy(
            src_ref=part.at[i, j, 1],
            dst_ref=pair_in.at[i, j],
            send_sem=p_send.at[i, j],
            recv_sem=p_recv.at[i, j],
            device_id=(mate[1], z),
            device_id_type=MESH,
        )

    def z_copy(i, j):
        zt = flip(chip, j, zbits)
        k = differ(z, zt, zbits)
        return zt, pltpu.make_async_remote_copy(
            src_ref=summed.at[i, j],
            dst_ref=z_in.at[k, i],
            send_sem=z_send.at[i, j],
            recv_sem=z_recv.at[k, i],
            device_id=(r, zt),
            device_id_type=MESH,
        )

    def put(i, j, value):
        part[i, j, 0] = value[:block]
        part[i, j, 1] = value[block:]
        pair_copy(i, j).start()

    def late_copy(i, j):
        return pltpu.make_async_remote_copy(
            src_ref=summed.at[i, j],
            dst_ref=late_in.at[i, i ^ j],
            send_sem=l_send.at[i, i ^ j],
            recv_sem=l_recv.at[i, i ^ j],
            device_id=(mate[2 * i], z),
            device_id_type=MESH,
        )

    def z_late_copy(m):
        zt = flip(chip, m, zbits)
        k = differ(z, zt, zbits)
        return zt, pltpu.make_async_remote_copy(
            src_ref=late_sum.at[m],
            dst_ref=zl_in.at[k],
            send_sem=zl_send.at[m],
            recv_sem=zl_recv.at[k],
            device_id=(r, zt),
            device_id_type=MESH,
        )

    def plane_copy(i):
        return pltpu.make_async_remote_copy(
            src_ref=plane_out.at[i],
            dst_ref=plane_in.at[i],
            send_sem=g_send.at[i],
            recv_sem=g_recv.at[i],
            device_id=(mate[2 * i], z),
            device_id_type=MESH,
        )

    def finish(i, j):
        pair_copy(i, j).wait_recv()
        summed[i, j, :, :block] = part[i, j, 0, :, :block] + pair_in[i, j, :, block:]
        summed[i, j, :, block:] = part[i, j, 0, :, block:] + pair_in[i, j, :, :block]
        if i == last or j == last:
            if i > 0:
                late_copy(i, j).start()
        else:
            zt, copy = z_copy(i, j)

            @pl.when(zt != z)
            def _():
                copy.start()

    def product(i, g, at):
        return (
            dot_t(hi[i, :, at], hi[g, :, at])
            + dot_t(hi[i, :, at], lo[g, :, at])
            + dot_t(lo[i, :, at], hi[g, :, at])
        )

    for g in range(last):
        for k in (2 * g, 2 * g + 1):
            if k == 0:
                own.wait()
            else:
                a2a[k][0].wait_recv()
            split(k, range(per))
        fresh = []
        for i in range(g + 1):
            value = product(i, g, slice(None))
            put(i, g, value)
            fresh.append((i, g))
            if i < g:
                put(g, i, value.T)
                fresh.append((g, i))
        if g == 0:
            for k in order:
                if 2 <= k < 2 * last:
                    a2a[k][0].wait_send()
            for p in range(per):
                for k in (2 * last, 2 * last + 1):
                    a2a[k][p].start()
        for i, j in fresh:
            finish(i, j)

    for p in range(per):
        for k in (2 * last, 2 * last + 1):
            a2a[k][p].wait_recv()
            split(k, (p,))
        at = slice(p * depth, (p + 1) * depth)
        waiting = []
        for i in range(chips):
            value = product(i, last, at)
            if p > 0:
                value = value + acc[i]
            if p < per - 1:
                acc[i] = value
                continue
            fresh = [(i, last)]
            if i < last:
                put(last, i, value.T)
                fresh.insert(0, (last, i))
            put(i, last, value)
            for pair in waiting:
                finish(*pair)
            waiting = fresh
        for pair in waiting:
            finish(*pair)

    for m in range(last, -1, -1):
        sources = {last, last ^ m}
        total = None
        for i in sorted(sources):
            if i == 0:
                piece = summed[0, last]
            else:
                late_copy(i, i ^ m).wait_recv()
                piece = late_in[i, m]
            total = piece if total is None else total + piece
        late_sum[m] = total
        zt, copy = z_late_copy(m)

        @pl.when(zt != z)
        def _():
            copy.start()

    for i in list(range(1, last)) + [0]:
        @pl.when(mine < last)
        def _():
            total = summed[i, mine]
            for k in range(1, cols):
                pltpu.make_async_remote_copy(
                    src_ref=summed.at[i, 0],
                    dst_ref=z_in.at[k, i],
                    send_sem=z_send.at[i, 0],
                    recv_sem=z_recv.at[k, i],
                    device_id=(r, flip(z, k, zbits)),
                    device_id_type=MESH,
                ).wait_recv()
                total = total + z_in[k, i]
            plane_out[i] = total

        @pl.when(mine == last)
        def _():
            plane_out[i] = jnp.zeros((block, 2 * block), jnp.float32)

        if i > 0:
            plane_copy(i).start()

    total = plane_out[0]
    for i in range(1, last):
        plane_copy(i).wait_recv()
        total = total + plane_in[i]
    total = total + late_sum[mine]
    for k in range(1, cols):
        pltpu.make_async_remote_copy(
            src_ref=late_sum.at[0],
            dst_ref=zl_in.at[k],
            send_sem=zl_send.at[0],
            recv_sem=zl_recv.at[k],
            device_id=(r, flip(z, k, zbits)),
            device_id_type=MESH,
        ).wait_recv()
        total = total + zl_in[k]
    total = total * scale
    first = pl.multiple_of(core * block, block)
    second = pl.multiple_of((1 - core) * block, block)
    gram[:, pl.ds(first, block)] = total[:, :block]
    gram[:, pl.ds(second, block)] = total[:, block:]

    value = lax.dot_general(
        fac[...], gram[...], (((0,), (0,)), ((), ())),
        precision=lax.Precision.HIGHEST, preferred_element_type=jnp.float32,
    )
    share = value.shape[0] // rows
    for k in range(rows):
        term[k] = value[k * share:(k + 1) * share]

    def term_copy(k):
        return pltpu.make_async_remote_copy(
            src_ref=term.at[mate[k]],
            dst_ref=term_in.at[k],
            send_sem=t_send.at[k],
            recv_sem=t_recv.at[k],
            device_id=(mate[k], z),
            device_id_type=MESH,
        )

    for k in range(rows - 1, 0, -1):
        term_copy(k).start()
    total = term[r]
    for k in range(1, rows):
        term_copy(k).wait_recv()
        total = total + term_in[k]
    proj[...] = total.T

    for k in range(1, rows):
        if k < 2 or k >= 2 * last:
            for copy in a2a[k]:
                copy.wait_send()
        term_copy(k).wait_send()
    for i in range(chips):
        for j in range(chips):
            pair_copy(i, j).wait_send()
            if i < last and j < last:
                zt, copy = z_copy(i, j)

                @pl.when(zt != z)
                def _():
                    copy.wait_send()
            elif i > 0:
                late_copy(i, j).wait_send()
        if 0 < i < last:
            plane_copy(i).wait_send()
        zt, copy = z_late_copy(i)

        @pl.when(zt != z)
        def _():
            copy.wait_send()


def fused(pixels, factor):
    rows, cols = lax.axis_size("row"), lax.axis_size("col")
    views, colours, block, depth = pixels.shape
    count = views * colours
    per = count // rows
    chips = rows // 2
    rank = factor.shape[1]
    scale = 1.0 / (count * depth * cols)
    vmem, dma = pltpu.VMEM, pltpu.SemaphoreType.DMA
    f32 = jnp.float32
    return pl.pallas_call(
        functools.partial(kernel, rows, cols, scale),
        out_shape=(
            jax.ShapeDtypeStruct((block, 2 * block), f32),
            jax.ShapeDtypeStruct((2 * block, rank // rows), f32),
        ),
        in_specs=[pl.BlockSpec(memory_space=pl.ANY), pl.BlockSpec(memory_space=pltpu.VMEM)],
        out_specs=(pl.BlockSpec(memory_space=pltpu.VMEM), pl.BlockSpec(memory_space=pltpu.VMEM)),
        scratch_shapes=[
            vmem((rows, per, block, depth), f32),
            vmem((chips, 2 * block, per * depth), jnp.bfloat16),
            vmem((chips, 2 * block, per * depth), jnp.bfloat16),
            vmem((chips, chips, 2, block, 2 * block), f32),
            vmem((chips, chips, block, 2 * block), f32),
            vmem((chips, chips, block, 2 * block), f32),
            vmem((cols, chips, block, 2 * block), f32),
            vmem((chips, block, 2 * block), f32),
            vmem((chips, block, 2 * block), f32),
            vmem((chips, chips, block, 2 * block), f32),
            vmem((chips, block, 2 * block), f32),
            vmem((cols, block, 2 * block), f32),
            vmem((chips, 2 * block, 2 * block), f32),
            vmem((rows, rank // rows, 2 * block), f32),
            vmem((rows, rank // rows, 2 * block), f32),
            dma,
            dma((rows,)), dma((rows,)),
            dma((2, per)), dma((2, per)),
            dma((chips, chips)), dma((chips, chips)),
            dma((chips, chips)), dma((cols, chips)),
            dma((chips,)), dma((chips,)),
            dma((chips, chips)), dma((chips, chips)),
            dma((chips,)), dma((cols,)),
            dma((rows,)), dma((rows,)),
        ],
        compiler_params=pltpu.CompilerParams(
            collective_id=0, has_side_effects=True, vmem_limit_bytes=56 * 1024 * 1024
        ),
    )(pixels.reshape(count, block, depth), factor)


def pair_rows(own, others):
    return jnp.einsum(
        "vciw,vcjw->ij", own, others, precision=lax.Precision.HIGHEST, preferred_element_type=jnp.float32
    )


def general(pixels, factor):
    col_count = lax.axis_size("col")
    row_count = lax.axis_size("row")
    weight_scale = 1.0 / (pixels.shape[0] * pixels.shape[1] * pixels.shape[3] * col_count)
    row_block = pixels.shape[2]
    slices = lax.all_to_all(pixels, "row", split_axis=3, concat_axis=2, tiled=True)
    partial_value = pair_rows(slices, slices) * weight_scale
    width = partial_value.shape[0] // col_count
    arranged = partial_value.reshape(row_count, row_block, col_count, width)
    arranged = jnp.transpose(arranged, (0, 2, 1, 3)).reshape(row_count * col_count * row_block, width)
    block = lax.psum_scatter(arranged, ("row", "col"), scatter_dimension=0, tiled=True)
    term = lax.dot_general(
        block, factor, (((0,), (0,)), ((), ())),
        precision=lax.Precision.HIGHEST, preferred_element_type=jnp.float32,
    )
    summed_term = lax.psum(term, "row")
    share = summed_term.shape[1] // row_count
    projected = lax.dynamic_slice_in_dim(summed_term, lax.axis_index("row") * share, share, 1)
    return (block, projected)


def shards(pixels, factor):
    rows, cols = lax.axis_size("row"), lax.axis_size("col")
    views, colours, block, depth = pixels.shape
    fits = (
        rows == 2 * cols
        and rows >= 4
        and rows & (rows - 1) == 0
        and (views * colours) % rows == 0
        and block % 128 == 0
        and depth % 128 == 0
        and factor.shape[1] % (8 * rows) == 0
        and 8 * rows * block * (views * colours // rows) * depth <= 16 * 1024 * 1024
    )
    return (fused if fits else general)(pixels, factor)


def solution(mesh):
    in_specs = (P(None, None, "row", "col"), P("row", None))
    out_specs = (P("row", "col"), P("col", "row"))
    return jax.shard_map(shards, mesh=mesh, in_specs=in_specs, out_specs=out_specs, check_vma=False)
```
